32 devices in a mesh: section: 2 (over x), dp: 4 (over z), tensor: 4 (over y, core).
Axes of the slice: x: 2, y: 2, z: 4, core: 2. Of those that a mesh axis runs over, the one named last changes fastest.
Arguments:
- layer_input: bfloat16 [1024, 1024], P('dp'), may hold values from -6 to 6
- output_cotangent: bfloat16 [1024, 1024], P('dp'), may hold values from -6 to 6
- positions: int32 [1024], P('dp'), may hold values from 0 to 255, as said below
- norm_first: float32 [2, 1024], P('section'), may hold values from 0.5 to 1.5
- query_weight: bfloat16 [2, 1024, 512], P('section', None, 'tensor'), may hold values from -0.1875 to 0.1875
- key_projection_weight: bfloat16 [2, 1024, 128], P('section'), may hold values from -0.1875 to 0.1875
- value_projection_weight: bfloat16 [2, 1024, 128], P('section'), may hold values from -0.1875 to 0.1875
- output_weight: bfloat16 [2, 512, 1024], P('section', 'tensor'), may hold values from -1 to 1
- mixer_gate: bfloat16 [2, 1024, 1536], P('section', None, 'tensor'), may hold values from -0.1875 to 0.1875
- mixer_input: bfloat16 [2, 1024, 1536], P('section', None, 'tensor'), may hold values from -0.1875 to 0.1875
- state_input: bfloat16 [2, 1024, 128], P('section'), may hold values from -0.0625 to 0.0625
- state_output: bfloat16 [2, 1024, 128], P('section'), may hold values from -0.0625 to 0.0625
- step_weight: bfloat16 [2, 1024, 24], P('section', None, 'tensor'), may hold values from -0.09375 to 0.09375
- step_bias: float32 [2, 24], P('section', 'tensor'), may hold values from -4 to -1
- decay_log: float32 [2, 24], P('section', 'tensor'), may hold values from -3 to 1
- skip_scale: float32 [2, 24], P('section', 'tensor'), may hold values from 0.5 to 1.5
- mixer_output: bfloat16 [2, 1536, 1024], P('section', 'tensor'), may hold values from -0.15625 to 0.15625
- norm_second: float32 [2, 1024], P('section'), may hold values from 0.5 to 1.5
- hidden_gate: bfloat16 [2, 1024, 2048], P('section', None, 'tensor'), may hold values from -0.1875 to 0.1875
- hidden_up: bfloat16 [2, 1024, 2048], P('section', None, 'tensor'), may hold values from -0.1875 to 0.1875
- hidden_down: bfloat16 [2, 2048, 1024], P('section', 'tensor'), may hold values from -0.125 to 0.125
Outputs:
- block_output: bfloat16 [2, 1024, 1024], P('section', 'dp')
- input_gradient: bfloat16 [2, 1024, 1024], P('section', 'dp')
- grad_norm_first: float32 [2, 1024], P('section')
- grad_query_weight: float32 [2, 1024, 512], P('section', None, 'tensor')
- grad_key_weight: float32 [2, 1024, 128], P('section')
- grad_value_weight: float32 [2, 1024, 128], P('section')
- grad_output_weight: float32 [2, 512, 1024], P('section', 'tensor')
- grad_mixer_gate: float32 [2, 1024, 1536], P('section', None, 'tensor')
- grad_mixer_input: float32 [2, 1024, 1536], P('section', None, 'tensor')
- grad_state_input: float32 [2, 1024, 128], P('section')
- grad_state_output: float32 [2, 1024, 128], P('section')
- grad_step_weight: float32 [2, 1024, 24], P('section', None, 'tensor')
- grad_step_bias: float32 [2, 24], P('section', 'tensor')
- grad_decay_log: float32 [2, 24], P('section', 'tensor')
- grad_skip_scale: float32 [2, 24], P('section', 'tensor')
- grad_mixer_output: float32 [2, 1536, 1024], P('section', 'tensor')
- grad_norm_second: float32 [2, 1024], P('section')
- grad_hidden_gate: float32 [2, 1024, 2048], P('section', None, 'tensor')
- grad_hidden_up: float32 [2, 1024, 2048], P('section', None, 'tensor')
- grad_hidden_down: float32 [2, 2048, 1024], P('section', 'tensor')
The draws below stay inside these ranges and needn't reach their ends.
Inputs may be any that keep to these rules, and one draw needn't show every extreme that they name: positions count from 0 at a document's first token and rise by one a token; each aligned run of 256 tokens is one sequence whose first token starts a document.
All inputs are finite; a program needn't handle non-finite values.
Results may differ from the reference program's by a relative error of at most 0.035.
Values may be sent and summed in bfloat16 or wider, within the bound.
A program may use at most 128 MiB of HBM per device.

```python
import jax
import jax.numpy as jnp
from jax import lax

MODEL_DIM = 1024
QUERY_HEADS = 8
KEY_VALUE_HEADS = 2
HEAD_DIM = 64
HM = 24
MD = 64
NS = 128
FF = 2048
LEN = 256
TOKENS = 1024
SECTION_LAYERS = 2


def draw_positions(key, part):
    sequence_count = TOKENS // LEN
    start_marks = jax.random.randint(key, (sequence_count, LEN), 0, 40) == 0
    token_index = jnp.arange(LEN, dtype=jnp.int32)
    single = (jnp.arange(sequence_count, dtype=jnp.int32) % 4 == 0)[:, None]
    starts = start_marks & jnp.logical_not(single) | (token_index[None, :] == 0)
    last_start = lax.cummax(jnp.where(starts, token_index[None, :], 0), axis=1)
    return (token_index[None, :] - last_start).reshape(TOKENS).astype(jnp.int32)


def block_levels(rng, extent, shards, smallest, largest):
    factor_of, own = 1.0, jax.random.fold_in(rng, 6)
    for axis_at, parts in shards:
        steps = jnp.exp(jax.random.uniform(jax.random.fold_in(own, axis_at), (parts,), jnp.float32, smallest / len(shards), largest / len(shards)))
        factor_of = factor_of * jnp.repeat(steps, extent[axis_at] // parts).reshape([-1 if axis == axis_at else 1 for axis in range(len(extent))])
    return factor_of


def normal_values(own_key, extent, deviation, most, split=(), kind=jnp.bfloat16):
    result = jax.random.normal(own_key, extent, jnp.float32) * deviation
    if len(split) > 0:
        result = block_levels(own_key, extent, split, -0.22, 0.18) * result
    return jnp.clip(result, min=-most, max=most).astype(kind)


def setup_inputs(seed: int = 0) -> dict:
    keys = jax.random.split(jax.random.key(seed), 22)
    layer_input = normal_values(keys[0], (TOKENS, MODEL_DIM), 1.0, 6.0, ((0, 4),))
    output_cotangent = normal_values(keys[1], (TOKENS, MODEL_DIM), 1.0, 6.0, ((0, 4),))
    positions = draw_positions(jax.random.fold_in(keys[21], 71), 0)
    norm_first = jnp.clip(1.0 + 0.1 * jax.random.normal(keys[3], (SECTION_LAYERS, MODEL_DIM), jnp.float32), 0.5, 1.5)
    query_weight = normal_values(keys[4], (SECTION_LAYERS, MODEL_DIM, QUERY_HEADS * HEAD_DIM), MODEL_DIM ** -0.5, 0.1875, ((0, 2), (2, 4)))
    key_projection_weight = normal_values(keys[5], (SECTION_LAYERS, MODEL_DIM, KEY_VALUE_HEADS * HEAD_DIM), MODEL_DIM ** -0.5, 0.1875, ((0, 2),))
    value_projection_weight = normal_values(keys[6], (SECTION_LAYERS, MODEL_DIM, KEY_VALUE_HEADS * HEAD_DIM), MODEL_DIM ** -0.5, 0.1875, ((0, 2),))
    output_weight = normal_values(keys[7], (SECTION_LAYERS, QUERY_HEADS * HEAD_DIM, MODEL_DIM), (QUERY_HEADS * HEAD_DIM // 16) ** -0.5, 1.0, ((0, 2), (1, 4)))
    mixer_gate = normal_values(keys[8], (SECTION_LAYERS, MODEL_DIM, HM * MD), MODEL_DIM ** -0.5, 0.1875, ((0, 2), (2, 4)))
    mixer_input = normal_values(keys[9], (SECTION_LAYERS, MODEL_DIM, HM * MD), MODEL_DIM ** -0.5, 0.1875, ((0, 2), (2, 4)))
    state_input = normal_values(keys[10], (SECTION_LAYERS, MODEL_DIM, NS), (MODEL_DIM * 8) ** -0.5, 0.0625, ((0, 2),))
    state_output = normal_values(keys[11], (SECTION_LAYERS, MODEL_DIM, NS), (MODEL_DIM * 8) ** -0.5, 0.0625, ((0, 2),))
    step_weight = normal_values(keys[12], (SECTION_LAYERS, MODEL_DIM, HM), (MODEL_DIM * 4) ** -0.5, 0.09375, ((0, 2), (2, 4)))
    step_bias = jnp.clip(-4.0 + 3.0 * jax.random.uniform(keys[13], (SECTION_LAYERS, HM), jnp.float32) ** block_levels(keys[13], (SECTION_LAYERS, HM), ((0, 2), (1, 4)), -0.2, 0.2), -4.0, -1.0)
    decay_log = jnp.clip(-3.0 + 4.0 * jax.random.uniform(keys[14], (SECTION_LAYERS, HM), jnp.float32) ** block_levels(keys[14], (SECTION_LAYERS, HM), ((0, 2), (1, 4)), -0.2, 0.2), -3.0, 1.0)
    skip_scale = jnp.clip(0.5 + 1.0 * jax.random.uniform(keys[15], (SECTION_LAYERS, HM), jnp.float32) ** block_levels(keys[15], (SECTION_LAYERS, HM), ((0, 2), (1, 4)), -0.2, 0.2), 0.5, 1.5)
    mixer_output = normal_values(keys[16], (SECTION_LAYERS, HM * MD, MODEL_DIM), (HM * MD) ** -0.5, 0.15625, ((0, 2), (1, 4)))
    norm_second = jnp.clip(1.0 + 0.1 * jax.random.normal(keys[17], (SECTION_LAYERS, MODEL_DIM), jnp.float32), 0.5, 1.5)
    hidden_gate = normal_values(keys[18], (SECTION_LAYERS, MODEL_DIM, FF), MODEL_DIM ** -0.5, 0.1875, ((0, 2), (2, 4)))
    hidden_up = normal_values(keys[19], (SECTION_LAYERS, MODEL_DIM, FF), MODEL_DIM ** -0.5, 0.1875, ((0, 2), (2, 4)))
    hidden_down = normal_values(keys[20], (SECTION_LAYERS, FF, MODEL_DIM), FF ** -0.5, 0.125, ((0, 2), (1, 4)))
    return dict(layer_input=layer_input, output_cotangent=output_cotangent, positions=positions, norm_first=norm_first, query_weight=query_weight, key_projection_weight=key_projection_weight, value_projection_weight=value_projection_weight, output_weight=output_weight, mixer_gate=mixer_gate, mixer_input=mixer_input, state_input=state_input, state_output=state_output, step_weight=step_weight, step_bias=step_bias, decay_log=decay_log, skip_scale=skip_scale, mixer_output=mixer_output, norm_second=norm_second, hidden_gate=hidden_gate, hidden_up=hidden_up, hidden_down=hidden_down)


EPS = 1e-06
highest = lax.Precision.HIGHEST

def bdot(left, right):
    return jnp.dot(left.astype(jnp.float32), right.astype(jnp.float32), precision=highest)

def rms_scale(layer_token_rows, gain):
    return layer_token_rows * lax.rsqrt(lax.optimization_barrier(jnp.mean(layer_token_rows * layer_token_rows, axis=-1, keepdims=True)) + EPS) * gain

def visible(positions):
    token_index = jnp.arange(positions.shape[0], dtype=jnp.int32)
    return (token_index[None, :] <= token_index[:, None]) & (token_index[None, :] >= token_index[:, None] - positions[:, None])

def silu_product(gate_pre, upper_part):
    return jax.nn.silu(gate_pre) * upper_part

def mixer_core(mixer_in, gate_z, state_in, state_out, step_raw, step_bias, decay_log, skip_scale, causal_visible_mask):
    length = mixer_in.shape[0]
    head_count = step_bias.shape[0]
    head_width = mixer_in.shape[1] // head_count
    step_size = jax.nn.softplus(step_raw + step_bias)
    log_decay = jnp.cumsum(step_size * -jnp.exp(decay_log), axis=0).T
    spread = log_decay[:, :, None] - log_decay[:, None, :]
    wide_mask = causal_visible_mask[None]
    decay_factor = jnp.where(wide_mask, jnp.exp(jnp.where(wide_mask, spread, 0.0)), 0.0)
    state_inner = jnp.dot(state_out, state_in.T, precision=highest)
    mixing = state_inner[None] * decay_factor * step_size.T[:, None, :]
    by_head = mixer_in.reshape(length, head_count, head_width).transpose(1, 0, 2)
    mixed_rows = jnp.einsum('hts,hsp->htp', mixing, by_head, precision=highest) + skip_scale[:, None, None] * by_head
    return mixed_rows.transpose(1, 0, 2).reshape(length, head_count * head_width) * jax.nn.silu(gate_z)

def heads_first(layer_token_rows, head_width):
    return layer_token_rows.reshape(layer_token_rows.shape[0], layer_token_rows.shape[1] // head_width, head_width).transpose(1, 0, 2)

def rows_first(by_head):
    return by_head.transpose(1, 0, 2).reshape(by_head.shape[1], by_head.shape[0] * by_head.shape[2])

def attention_scores(query_matrix, key_matrix_rows, causal_visible_mask, query_group_width):
    by_query = heads_first(query_matrix, HEAD_DIM).astype(jnp.float32)
    by_key = jnp.repeat(heads_first(key_matrix_rows, HEAD_DIM), query_group_width, axis=0).astype(jnp.float32)
    scores = jnp.einsum('hqd,hkd->hqk', by_query, by_key, precision=highest) * HEAD_DIM ** (-0.5)
    return (jnp.where(causal_visible_mask[None], scores, -1e+30), by_query, by_key)

def attention_forward(query_matrix, key_matrix_rows, value_matrix_rows, causal_visible_mask, query_group_width):
    scores, by_query, by_key = attention_scores(query_matrix, key_matrix_rows, causal_visible_mask, query_group_width)
    row_top = lax.optimization_barrier(jnp.max(scores, axis=-1, keepdims=True))
    logarithm_total = row_top + jnp.log(lax.optimization_barrier(jnp.sum(jnp.exp(scores - row_top), axis=-1, keepdims=True)))
    soft_weights = jnp.exp(scores - logarithm_total).astype(jnp.bfloat16)
    by_value = jnp.repeat(heads_first(value_matrix_rows, HEAD_DIM), query_group_width, axis=0).astype(jnp.float32)
    context = jnp.einsum('hqk,hkd->hqd', soft_weights.astype(jnp.float32), by_value, precision=highest)
    return (rows_first(context).astype(jnp.bfloat16), logarithm_total)

def attention_reverse_pass(query_matrix, key_matrix_rows, value_matrix_rows, logarithm_total, context_gradient, causal_visible_mask, query_group_width):
    scores, by_query, by_key = attention_scores(query_matrix, key_matrix_rows, causal_visible_mask, query_group_width)
    probabilities = jnp.exp(scores - logarithm_total)
    by_value = jnp.repeat(heads_first(value_matrix_rows, HEAD_DIM), query_group_width, axis=0).astype(jnp.float32)
    by_grad = heads_first(context_gradient, HEAD_DIM).astype(jnp.float32)
    prob_grad = jnp.einsum('hqd,hkd->hqk', by_grad, by_value, precision=highest)
    row_delta = lax.optimization_barrier(jnp.sum(probabilities * prob_grad, axis=-1, keepdims=True))
    score_grad = (probabilities * (prob_grad - row_delta) * HEAD_DIM ** (-0.5)).astype(jnp.bfloat16).astype(jnp.float32)
    query_gradient = jnp.einsum('hqk,hkd->hqd', score_grad, by_key, precision=highest)
    kv_heads = by_key.shape[0] // query_group_width
    key_gradient = jnp.einsum('hqk,hqd->hkd', score_grad, by_query, precision=highest)
    key_gradient = key_gradient.reshape(kv_heads, query_group_width, key_gradient.shape[1], key_gradient.shape[2]).sum(axis=1)
    value_gradient = jnp.einsum('hqk,hqd->hkd', probabilities.astype(jnp.bfloat16).astype(jnp.float32), by_grad, precision=highest)
    value_gradient = value_gradient.reshape(kv_heads, query_group_width, value_gradient.shape[1], value_gradient.shape[2]).sum(axis=1)
    return (rows_first(query_gradient), rows_first(key_gradient), rows_first(value_gradient))

def mixer_saved_values(layer_token_rows, parameters, key_cols, value_cols, causal_visible_mask, query_group_width):
    normed_input = rms_scale(layer_token_rows, parameters[0]).astype(jnp.bfloat16)
    query_matrix = bdot(normed_input, parameters[1]).astype(jnp.bfloat16)
    key_matrix_rows = bdot(normed_input, key_cols).astype(jnp.bfloat16)
    value_matrix_rows = bdot(normed_input, value_cols).astype(jnp.bfloat16)
    context, logarithm_total = attention_forward(query_matrix, key_matrix_rows, value_matrix_rows, causal_visible_mask, query_group_width)
    mixer_args = tuple((bdot(normed_input, parameters[weight_slot]) for weight_slot in (6, 5, 7, 8, 9)))
    gated = mixer_core(mixer_args[0], mixer_args[1], mixer_args[2], mixer_args[3], mixer_args[4], parameters[10], parameters[11], parameters[12], causal_visible_mask)
    mixer_rows = gated.astype(jnp.bfloat16)
    return (normed_input, query_matrix, key_matrix_rows, value_matrix_rows, context, logarithm_total, mixer_args, mixer_rows)

def ffn_locals(middle, parameters):
    normed = rms_scale(middle, parameters[14]).astype(jnp.bfloat16)
    gate_pre = bdot(normed, parameters[15])
    upper_part = bdot(normed, parameters[16])
    hidden = silu_product(gate_pre, upper_part).astype(jnp.bfloat16)
    return (normed, gate_pre, upper_part, hidden)

def layer_middle(layer_token_rows, parameters, causal_visible_mask):
    gradient_parts = mixer_saved_values(layer_token_rows, parameters, parameters[2], parameters[3], causal_visible_mask, QUERY_HEADS // KEY_VALUE_HEADS)
    middle = layer_token_rows + bdot(gradient_parts[4], parameters[4]) + bdot(gradient_parts[7], parameters[13])
    return (gradient_parts, middle)

def layer_forward(layer_token_rows, parameters, causal_visible_mask):
    gradient_parts, middle = layer_middle(layer_token_rows, parameters, causal_visible_mask)
    normed, gate_pre, upper_part, hidden = ffn_locals(middle, parameters)
    return (middle + bdot(hidden, parameters[17])).astype(jnp.bfloat16)

def layer_backward(layer_token_rows, parameters, causal_visible_mask, out_grad):
    gradient_parts, middle = layer_middle(layer_token_rows, parameters, causal_visible_mask)
    normed_input, query_matrix, key_matrix_rows, value_matrix_rows, context, logarithm_total, mixer_args, mixer_rows = gradient_parts
    normed, gate_pre, upper_part, hidden = ffn_locals(middle, parameters)
    grad_down = bdot(hidden.T, out_grad)
    hidden_grad = bdot(out_grad, parameters[17].T)
    primal_out, silu_back = jax.vjp(silu_product, gate_pre, upper_part)
    gate_grad, upper_grad = silu_back(hidden_grad)
    gate_grad = gate_grad.astype(jnp.bfloat16)
    upper_grad = upper_grad.astype(jnp.bfloat16)
    grad_gate = bdot(normed.T, gate_grad)
    grad_up = bdot(normed.T, upper_grad)
    normed_grad = bdot(gate_grad, parameters[15].T) + bdot(upper_grad, parameters[16].T)
    primal_out, second_back = jax.vjp(rms_scale, middle, parameters[14])
    middle_part, grad_second = second_back(normed_grad)
    middle_grad = out_grad.astype(jnp.float32) + middle_part
    middle_low = middle_grad.astype(jnp.bfloat16)
    grad_output = bdot(context.T, middle_low)
    context_gradient = bdot(middle_low, parameters[4].T).astype(jnp.bfloat16)
    grad_mixer_out = bdot(mixer_rows.T, middle_low)
    mixer_grad = bdot(middle_low, parameters[13].T)
    query_gradient, key_gradient, value_gradient = attention_reverse_pass(query_matrix, key_matrix_rows, value_matrix_rows, logarithm_total, context_gradient, causal_visible_mask, QUERY_HEADS // KEY_VALUE_HEADS)

    def core_fixed(mixer_in, gate_z, state_in, state_out, step_raw, step_bias, decay_log, skip_scale):
        return mixer_core(mixer_in, gate_z, state_in, state_out, step_raw, step_bias, decay_log, skip_scale, causal_visible_mask)
    primal_out, core_back = jax.vjp(core_fixed, mixer_args[0], mixer_args[1], mixer_args[2], mixer_args[3], mixer_args[4], parameters[10], parameters[11], parameters[12])
    core_grads = core_back(mixer_grad)
    low_grads = [query_gradient.astype(jnp.bfloat16), key_gradient.astype(jnp.bfloat16), value_gradient.astype(jnp.bfloat16)]
    low_grads = low_grads + [core_grads[slot_number].astype(jnp.bfloat16) for slot_number in range(5)]
    weights_used = (parameters[1], parameters[2], parameters[3], parameters[6], parameters[5], parameters[7], parameters[8], parameters[9])
    proj_grads = [bdot(normed_input.T, grad_piece) for grad_piece in low_grads]
    act_grad = jnp.zeros(layer_token_rows.shape, jnp.float32)
    for grad_piece, weight in zip(low_grads, weights_used):
        act_grad = act_grad + bdot(grad_piece, weight.T)
    primal_out, first_back = jax.vjp(rms_scale, layer_token_rows, parameters[0])
    rows_part, grad_first = first_back(act_grad)
    input_grad = (middle_grad + rows_part).astype(jnp.bfloat16)
    grads = (grad_first, proj_grads[0], proj_grads[1], proj_grads[2], grad_output, proj_grads[4], proj_grads[3], proj_grads[5], proj_grads[6], proj_grads[7], core_grads[5], core_grads[6], core_grads[7], grad_mixer_out, grad_second, grad_gate, grad_up, grad_down)
    return (input_grad, grads)

def reference(layer_input, output_cotangent, positions, norm_first, query_weight, key_projection_weight, value_projection_weight, output_weight, mixer_gate, mixer_input, state_input, state_output, step_weight, step_bias, decay_log, skip_scale, mixer_output, norm_second, hidden_gate, hidden_up, hidden_down):
    stacked = (norm_first, query_weight, key_projection_weight, value_projection_weight, output_weight, mixer_gate, mixer_input, state_input, state_output, step_weight, step_bias, decay_log, skip_scale, mixer_output, norm_second, hidden_gate, hidden_up, hidden_down)
    sequence_count = layer_input.shape[0] // LEN
    seq_positions = positions.reshape(sequence_count, LEN)
    carried = layer_input.reshape(sequence_count, LEN, MODEL_DIM)
    layer_inputs = []
    block_outputs = []
    for layer_index in range(SECTION_LAYERS):
        parameters = tuple((weight[layer_index] for weight in stacked))
        layer_inputs.append(carried)

        def forward_one(seq_pair, parameters=parameters):
            return layer_forward(seq_pair[0].astype(jnp.float32), parameters, visible(seq_pair[1]))
        carried = lax.map(forward_one, (carried, seq_positions))
        block_outputs.append(carried)
    incoming = output_cotangent.reshape(sequence_count, LEN, MODEL_DIM)
    input_grads = [None] * SECTION_LAYERS
    weight_grads = [None] * SECTION_LAYERS
    for layer_index in reversed(range(SECTION_LAYERS)):
        parameters = tuple((weight[layer_index] for weight in stacked))

        def backward_one(running, triple, parameters=parameters):
            input_grad, grads = layer_backward(triple[0].astype(jnp.float32), parameters, visible(triple[1]), triple[2])
            return (tuple((sofar + addend for sofar, addend in zip(running, grads))), input_grad)
        zero_grads = tuple((jnp.zeros(weight.shape, jnp.float32) for weight in parameters))
        running, incoming = lax.scan(backward_one, zero_grads, (layer_inputs[layer_index], seq_positions, incoming))
        weight_grads[layer_index] = running
        input_grads[layer_index] = incoming
    outputs_all = jnp.stack(block_outputs).reshape(SECTION_LAYERS, sequence_count * LEN, MODEL_DIM)
    inputs_all = jnp.stack(input_grads).reshape(SECTION_LAYERS, sequence_count * LEN, MODEL_DIM)
    grads_all = [jnp.stack([weight_grads[layer_index][slot_number] for layer_index in range(SECTION_LAYERS)]) for slot_number in range(18)]
    return (outputs_all, inputs_all, grads_all[0], grads_all[1], grads_all[2], grads_all[3], grads_all[4], grads_all[5], grads_all[6], grads_all[7], grads_all[8], grads_all[9], grads_all[10], grads_all[11], grads_all[12], grads_all[13], grads_all[14], grads_all[15], grads_all[16], grads_all[17])
```

```python
import functools

import jax
import jax.numpy as jnp
from jax import lax
from jax.experimental import pallas as pl
from jax.experimental.pallas import tpu as pltpu
from jax.sharding import PartitionSpec as P

QUERY_HEADS = 8
KEY_VALUE_HEADS = 2
HEAD_DIM = 64
LANES = 128
EPS = 1e-06
f32 = jnp.float32
bf16 = jnp.bfloat16
highest = lax.Precision.HIGHEST
VMEM = pltpu.VMEM


def dot(a, b):
    return jnp.dot(a, b, preferred_element_type=f32)


def dot_nt(a, b):
    return lax.dot_general(a, b, (((1,), (1,)), ((), ())), preferred_element_type=f32)


def dot_tn(a, b):
    return lax.dot_general(a, b, (((0,), (0,)), ((), ())), preferred_element_type=f32)


def tensor_sum_kernel(count, x_ref, out_ref, near, half, far, s_sem, r_sem, fs_sem, fr_sem):
    rows = x_ref.shape[0] // 2
    chips = count // 2
    me = lax.axis_index("tensor")
    core = lax.rem(me, 2)
    chip = lax.div(me, 2)
    mate = chip * 2 + (1 - core)
    far_ids = [lax.rem(chip + k, chips) * 2 + core for k in range(1, chips)]
    barrier = pltpu.get_barrier_semaphore()
    for peer in [mate] + far_ids:
        pl.semaphore_signal(
            barrier, inc=1, device_id={"tensor": peer}, device_id_type=pl.DeviceIdType.MESH
        )
    pl.semaphore_wait(barrier, chips)
    own = pl.ds(pl.multiple_of(core * rows, rows), rows)
    other = pl.ds(pl.multiple_of((1 - core) * rows, rows), rows)

    def copy(src, dst, send, recv, peer):
        return pltpu.make_async_remote_copy(
            src_ref=src,
            dst_ref=dst,
            send_sem=send,
            recv_sem=recv,
            device_id={"tensor": peer},
            device_id_type=pl.DeviceIdType.MESH,
        )

    first = copy(x_ref.at[other], near, s_sem.at[0], r_sem.at[0], mate)
    first.start()
    first.wait()
    half[...] = (x_ref[own, :].astype(f32) + near[...].astype(f32)).astype(bf16)
    across = [
        copy(half, far.at[k], fs_sem.at[k], fr_sem.at[k], far_ids[k]) for k in range(chips - 1)
    ]
    for c in across:
        c.start()
    for c in across:
        c.wait()
    total = half[...].astype(f32)
    for k in range(chips - 1):
        total = total + far[k].astype(f32)
    out_ref[own, :] = total.astype(bf16)
    last = copy(out_ref.at[own], out_ref.at[own], s_sem.at[1], r_sem.at[1], mate)
    last.start()
    last.wait()


def tensor_sum(value, slot):
    count = lax.axis_size("tensor")
    value = value.astype(bf16)
    rows, cols = value.shape
    chips = count // 2
    return pl.pallas_call(
        functools.partial(tensor_sum_kernel, count),
        out_shape=jax.ShapeDtypeStruct((rows, cols), bf16),
        in_specs=[pl.BlockSpec(memory_space=VMEM)],
        out_specs=pl.BlockSpec(memory_space=VMEM),
        scratch_shapes=[
            VMEM((rows // 2, cols), bf16),
            VMEM((rows // 2, cols), bf16),
            VMEM((max(chips - 1, 1), rows // 2, cols), bf16),
            pltpu.SemaphoreType.DMA((2,)),
            pltpu.SemaphoreType.DMA((2,)),
            pltpu.SemaphoreType.DMA((max(chips - 1, 1),)),
            pltpu.SemaphoreType.DMA((max(chips - 1, 1),)),
        ],
        compiler_params=pltpu.CompilerParams(collective_id=slot, has_side_effects=True),
    )(value)


class Cols:
    def __init__(self, q, x, ns):
        self.q = q
        self.k = q
        self.v = q + HEAD_DIM
        self.x = q + 2 * HEAD_DIM
        self.z = self.x + x
        self.si = self.z + x
        self.so = self.si + ns
        self.st = self.so + ns
        self.end = self.st + LANES
        self.width = x
        self.ns = ns


def core_setup(pos_ref, proj_ref, small_ref, c):
    t = proj_ref.shape[0]
    row = lax.broadcasted_iota(jnp.int32, (t, t), 0)
    col = lax.broadcasted_iota(jnp.int32, (t, t), 1)
    seen = (col <= row) & (col >= row - pos_ref[...])
    biased = proj_ref[:, c.st : c.end] + small_ref[0:1, :]
    step = jnp.maximum(biased, 0.0) + jnp.log1p(jnp.exp(-jnp.abs(biased)))
    rate = jnp.exp(small_ref[1:2, :])
    lower = (col <= row).astype(f32)
    decay = jnp.dot(lower, -step * rate, preferred_element_type=f32, precision=highest)
    return seen, biased, step, rate, decay, row, col


def core_forward_kernel(c, heads, pos_ref, proj_ref, small_ref, ctx_ref, rows_ref, lse_ref):
    seen, biased, step, rate, decay, row, col = core_setup(pos_ref, proj_ref, small_ref, c)
    t = proj_ref.shape[0]
    k = proj_ref[:, c.k : c.k + HEAD_DIM].astype(bf16)
    v = proj_ref[:, c.v : c.v + HEAD_DIM].astype(bf16)
    lane = lax.broadcasted_iota(jnp.int32, (t, LANES), 1)
    lse = jnp.zeros((t, LANES), f32)
    for h in range(c.q // HEAD_DIM):
        at = slice(h * HEAD_DIM, (h + 1) * HEAD_DIM)
        s = dot_nt(proj_ref[:, at].astype(bf16), k) * HEAD_DIM ** (-0.5)
        s = jnp.where(seen, s, -1e30)
        top = jnp.max(s, axis=-1, keepdims=True)
        e = jnp.exp(s - top)
        total = jnp.sum(e, axis=-1, keepdims=True)
        lse = jnp.where(lane == h, top + jnp.log(total), lse)
        ctx_ref[:, at] = dot((e * (1.0 / total)).astype(bf16), v).astype(bf16)
    lse_ref[...] = lse
    decay_t = decay.T
    step_t = step.T
    inner = dot_nt(
        proj_ref[:, c.so : c.so + c.ns].astype(bf16), proj_ref[:, c.si : c.si + c.ns].astype(bf16)
    )
    inner = jnp.where(seen, inner, 0.0)
    p = c.width // heads
    for h in range(heads):
        at = slice(h * p, (h + 1) * p)
        spread = jnp.where(seen, decay[:, h : h + 1] - decay_t[h : h + 1, :], 0.0)
        mix = inner * jnp.exp(spread) * step_t[h : h + 1, :]
        x = proj_ref[:, c.x + h * p : c.x + (h + 1) * p]
        z = proj_ref[:, c.z + h * p : c.z + (h + 1) * p]
        y = dot(mix.astype(bf16), x.astype(bf16)) + small_ref[2:3, h : h + 1] * x
        rows_ref[:, at] = (y * z * jax.nn.sigmoid(z)).astype(bf16)


def core_backward_kernel(
    c, heads, pos_ref, proj_ref, small_ref, lse_ref, dctx_ref, dmix_ref, grad_ref, part_ref, colg
):
    seen, biased, step, rate, decay, row, col = core_setup(pos_ref, proj_ref, small_ref, c)
    t = proj_ref.shape[0]
    k = proj_ref[:, c.k : c.k + HEAD_DIM].astype(bf16)
    v = proj_ref[:, c.v : c.v + HEAD_DIM].astype(bf16)
    scale = HEAD_DIM ** (-0.5)
    dk = jnp.zeros((t, HEAD_DIM), f32)
    dv = jnp.zeros((t, HEAD_DIM), f32)
    for h in range(c.q // HEAD_DIM):
        at = slice(h * HEAD_DIM, (h + 1) * HEAD_DIM)
        q = proj_ref[:, at].astype(bf16)
        dctx = dctx_ref[:, at]
        s = jnp.where(seen, dot_nt(q, k) * scale, -1e30)
        prob = jnp.exp(s - lse_ref[:, h : h + 1])
        dp = dot_nt(dctx, v)
        delta = jnp.sum(prob * dp, axis=-1, keepdims=True)
        ds = (prob * (dp - delta) * scale).astype(bf16)
        grad_ref[:, at] = dot(ds, k).astype(bf16)
        dk = dk + dot_tn(ds, q)
        dv = dv + dot_tn(prob.astype(bf16), dctx)
    grad_ref[:, c.k : c.k + HEAD_DIM] = dk.astype(bf16)
    grad_ref[:, c.v : c.v + HEAD_DIM] = dv.astype(bf16)

    decay_t = decay.T
    step_t = step.T
    si = proj_ref[:, c.si : c.si + c.ns].astype(bf16)
    so = proj_ref[:, c.so : c.so + c.ns].astype(bf16)
    inner = jnp.where(seen, dot_nt(so, si), 0.0)
    lane = lax.broadcasted_iota(jnp.int32, (t, LANES), 1)
    lane_row = lax.broadcasted_iota(jnp.int32, (1, LANES), 1)
    colg[...] = jnp.zeros_like(colg)
    row_sum = jnp.zeros((t, LANES), f32)
    dskip = jnp.zeros((1, LANES), f32)
    dinner = jnp.zeros((t, t), f32)
    p = c.width // heads
    for h in range(heads):
        at = slice(h * p, (h + 1) * p)
        spread = jnp.where(seen, decay[:, h : h + 1] - decay_t[h : h + 1, :], 0.0)
        factor = jnp.where(seen, jnp.exp(spread), 0.0)
        timed = factor * step_t[h : h + 1, :]
        mix = (inner * timed).astype(bf16)
        x = proj_ref[:, c.x + h * p : c.x + (h + 1) * p]
        z = proj_ref[:, c.z + h * p : c.z + (h + 1) * p]
        skip = small_ref[2:3, h : h + 1]
        xl = x.astype(bf16)
        y = dot(mix, xl) + skip * x
        sig = jax.nn.sigmoid(z)
        dg = dmix_ref[:, at]
        dy = dg * z * sig
        dyl = dy.astype(bf16)
        grad_ref[:, c.z + h * p : c.z + (h + 1) * p] = (
            dg * y * sig * (1.0 + z * (1.0 - sig))
        ).astype(bf16)
        grad_ref[:, c.x + h * p : c.x + (h + 1) * p] = (dot_tn(mix, dyl) + skip * dy).astype(bf16)
        dskip = jnp.where(
            lane_row == h, jnp.sum(jnp.sum(dy * x, axis=0, keepdims=True), axis=1, keepdims=True), dskip
        )
        dm = dot_nt(dyl, xl)
        dinner = dinner + dm * timed
        g = dm * (inner * factor)
        colg[h : h + 1, :] = jnp.sum(g, axis=0, keepdims=True)
        e = g * step_t[h : h + 1, :]
        row_sum = jnp.where(lane == h, jnp.sum(e, axis=1, keepdims=True), row_sum)
    dinner = dinner.astype(bf16)
    grad_ref[:, c.so : c.so + c.ns] = dot(dinner, si).astype(bf16)
    grad_ref[:, c.si : c.si + c.ns] = dot_tn(dinner, so).astype(bf16)
    col_sum = colg[...].T
    ddecay = row_sum - step * col_sum
    upper = (col >= row).astype(f32)
    tail = jnp.dot(upper, ddecay, preferred_element_type=f32, precision=highest)
    dstep = col_sum - rate * tail
    draw = dstep * jax.nn.sigmoid(biased)
    grad_ref[:, c.st : c.end] = draw.astype(bf16)
    part_ref[...] = jnp.zeros_like(part_ref)
    part_ref[0:1, :] = jnp.sum(draw, axis=0, keepdims=True)
    part_ref[1:2, :] = jnp.sum(tail * (-step * rate), axis=0, keepdims=True)
    part_ref[2:3, :] = dskip


def whole_blocks(number):
    return [pl.BlockSpec(memory_space=VMEM)] * number


def core_forward(c, heads, positions, proj, small):
    t = proj.shape[0]
    return pl.pallas_call(
        functools.partial(core_forward_kernel, c, heads),
        out_shape=(
            jax.ShapeDtypeStruct((t, c.q), bf16),
            jax.ShapeDtypeStruct((t, c.width), bf16),
            jax.ShapeDtypeStruct((t, LANES), f32),
        ),
        in_specs=whole_blocks(3),
        out_specs=tuple(whole_blocks(3)),
        cost_estimate=pl.CostEstimate(flops=10**9, bytes_accessed=10**7, transcendentals=10**6),
    )(positions, proj, small)


def core_backward(c, heads, positions, proj, small, lse, dctx, dmix):
    t = proj.shape[0]
    return pl.pallas_call(
        functools.partial(core_backward_kernel, c, heads),
        out_shape=(
            jax.ShapeDtypeStruct((t, c.end), bf16),
            jax.ShapeDtypeStruct((8, LANES), f32),
        ),
        in_specs=whole_blocks(6),
        out_specs=tuple(whole_blocks(2)),
        scratch_shapes=[VMEM((LANES, t), f32)],
        cost_estimate=pl.CostEstimate(
            flops=2 * 10**9, bytes_accessed=2 * 10**7, transcendentals=10**6
        ),
    )(positions, proj, small, lse, dctx, dmix)


def shifted(value, axis, steps):
    count = lax.axis_size(axis)
    initial, last = (max(0, -steps), min(count, count - steps))
    return lax.ppermute(value, axis, [(source, source + steps) for source in range(initial, last)])


def rms(v):
    return v * lax.rsqrt(jnp.mean(v * v, axis=-1, keepdims=True) + EPS)


def rms_back(v, gain, grad):
    inverse = lax.rsqrt(jnp.mean(v * v, axis=-1, keepdims=True) + EPS)
    unit = v * inverse
    scaled = grad * gain
    back = inverse * (scaled - unit * jnp.mean(scaled * unit, axis=-1, keepdims=True))
    return back, jnp.sum(grad * unit, axis=0)


def layer_forward(low, w, c, heads, positions):
    rows = low.astype(f32)
    normed_input = (rms(rows) * w["n1"]).astype(bf16)
    proj = dot(normed_input, w["cat"])
    ctx, mixer_rows, lse = core_forward(c, heads, positions, proj, w["small"])
    local = dot(ctx, w["out"]) + dot(mixer_rows, w["mo"])
    middle = rows + tensor_sum(local, 0).astype(f32)
    normed = (rms(middle) * w["n2"]).astype(bf16)
    gate_pre = dot(normed, w["hg"])
    upper = dot(normed, w["hu"])
    hidden = (jax.nn.silu(gate_pre) * upper).astype(bf16)
    local = dot(hidden, w["hd"])
    result = (middle + tensor_sum(local, 0).astype(f32)).astype(bf16)
    saved = (rows, normed_input, proj, ctx, mixer_rows, lse, middle, normed, gate_pre, upper, hidden)
    return result, saved


def layer_backward(out_grad, saved, w, c, heads, positions, full):
    rows, normed_input, proj, ctx, mixer_rows, lse, middle, normed, gate_pre, upper, hidden = saved
    dhidden = dot_nt(out_grad, w["hd"])
    sig = jax.nn.sigmoid(gate_pre)
    dgate = (dhidden * upper * sig * (1.0 + gate_pre * (1.0 - sig))).astype(bf16)
    dupper = (dhidden * gate_pre * sig).astype(bf16)
    local = dot_nt(dgate, w["hg"]) + dot_nt(dupper, w["hu"])
    normed_grad = tensor_sum(local, 0).astype(f32)
    back, dn2 = rms_back(middle, w["n2"], normed_grad)
    middle_grad = out_grad.astype(f32) + back
    middle_low = middle_grad.astype(bf16)
    dctx = dot_nt(middle_low, w["out"]).astype(bf16)
    dmix = dot_nt(middle_low, w["mo"])
    grads, parts = core_backward(c, heads, positions, proj, w["small"], lse, dctx, dmix)
    local = dot_nt(grads, w["cat"]).astype(bf16)
    shared_sum = None
    if full:
        kv = jnp.where(w["pick"], jnp.tile(grads[:, c.k : c.k + HEAD_DIM], (1, KEY_VALUE_HEADS)), 0)
        vv = jnp.where(w["pick"], jnp.tile(grads[:, c.v : c.v + HEAD_DIM], (1, KEY_VALUE_HEADS)), 0)
        joint = jnp.concatenate([local, kv, vv, grads[:, c.si : c.st]], axis=1)
        joint = tensor_sum(joint, 1)
        act_grad = joint[:, : local.shape[1]].astype(f32)
        shared_sum = joint[:, local.shape[1] :]
    else:
        act_grad = tensor_sum(local, 0).astype(f32)
    back, dn1 = rms_back(rows, w["n1"], act_grad)
    input_grad = (middle_grad + back).astype(bf16)
    return input_grad, (dgate, dupper, middle_low, grads, parts, shared_sum, dn1, dn2)


def gather(value):
    return lax.all_gather(value, "dp", axis=0, tiled=True)


def shards(
    layer_input,
    output_cotangent,
    positions,
    norm_first,
    query_weight,
    key_projection_weight,
    value_projection_weight,
    output_weight,
    mixer_gate,
    mixer_input,
    state_input,
    state_output,
    step_weight,
    step_bias,
    decay_log,
    skip_scale,
    mixer_output,
    norm_second,
    hidden_gate,
    hidden_up,
    hidden_down,
):
    section = lax.axis_index("section")
    tensor_position = lax.axis_index("tensor")
    group = query_weight.shape[-1] // HEAD_DIM
    head = tensor_position * group // (QUERY_HEADS // KEY_VALUE_HEADS)
    heads = step_bias.shape[-1]
    c = Cols(query_weight.shape[-1], mixer_input.shape[-1], state_input.shape[-1])
    key_cols = lax.dynamic_slice_in_dim(key_projection_weight[0], head * HEAD_DIM, HEAD_DIM, axis=1)
    value_cols = lax.dynamic_slice_in_dim(
        value_projection_weight[0], head * HEAD_DIM, HEAD_DIM, axis=1
    )
    pad = LANES - heads
    cat = jnp.concatenate(
        [
            query_weight[0],
            key_cols,
            value_cols,
            mixer_input[0],
            mixer_gate[0],
            state_input[0],
            state_output[0],
            jnp.pad(step_weight[0], ((0, 0), (0, pad))),
        ],
        axis=1,
    )
    small = jnp.pad(
        jnp.concatenate([step_bias, decay_log, skip_scale], axis=0), ((0, 5), (0, pad))
    )
    kv_width = key_projection_weight.shape[-1]
    w = {
        "n1": norm_first[0],
        "n2": norm_second[0],
        "cat": cat,
        "small": small,
        "out": output_weight[0],
        "mo": mixer_output[0],
        "hg": hidden_gate[0],
        "hu": hidden_up[0],
        "hd": hidden_down[0],
        "pick": (jnp.arange(kv_width) // HEAD_DIM == head)[None, :],
    }
    pos = positions[:, None]
    first, unused = layer_forward(layer_input, w, c, heads, pos)
    incoming = shifted(first, "section", 1)
    low = jnp.where(section == 0, layer_input, incoming)
    block_output, saved = layer_forward(low, w, c, heads, pos)
    rows, normed_input, proj, ctx, mixer_rows, lse, middle, normed, gate_pre, upper, hidden = saved
    normed_input_all = gather(normed_input)
    normed_all = gather(normed)
    hidden_all = gather(hidden)
    mixed_all = gather(jnp.concatenate([ctx, mixer_rows], axis=1))

    sent, unused = layer_backward(output_cotangent, saved, w, c, heads, pos, False)
    incoming = shifted(sent, "section", -1)
    last_section = lax.axis_size("section") - 1
    out_grad = jnp.where(section == last_section, output_cotangent, incoming)
    out_grad_all = gather(out_grad)
    input_grad, extra = layer_backward(out_grad, saved, w, c, heads, pos, True)
    dgate, dupper, middle_low, grads, parts, shared_sum, dn1, dn2 = extra
    ffn_all = gather(jnp.concatenate([dgate, dupper], axis=1))
    middle_all = gather(middle_low)
    own = jnp.concatenate([grads[:, : c.q], grads[:, c.x : c.si], grads[:, c.st :]], axis=1)
    own_all = gather(own)
    width = shared_sum.shape[1]
    vectors = jnp.concatenate([dn1, dn2, parts[:3].reshape(-1)]).astype(bf16)
    extra_rows = -(-vectors.shape[0] // (width * 16)) * 16
    vectors = jnp.pad(vectors, (0, extra_rows * width - vectors.shape[0]))
    t = shared_sum.shape[0]
    tail_all = gather(jnp.concatenate([shared_sum, vectors.reshape(extra_rows, width)], axis=0))
    tail_all = tail_all.reshape(-1, t + extra_rows, width)
    shared_all = tail_all[:, :t].reshape(-1, width)
    summed = jnp.sum(tail_all[:, t:].astype(f32), axis=0).reshape(-1)
    d = dn1.shape[0]
    three = summed[2 * d : 2 * d + 3 * LANES].reshape(3, LANES)[:, :heads]

    grad_down = dot_tn(hidden_all, out_grad_all)
    f = dgate.shape[1]
    grad_gate = dot_tn(normed_all, ffn_all[:, :f])
    grad_up = dot_tn(normed_all, ffn_all[:, f:])
    grad_out = dot_tn(mixed_all[:, : c.q], middle_all)
    grad_mo = dot_tn(mixed_all[:, c.q :], middle_all)
    q, x, ns = c.q, c.width, c.ns
    grad_query = dot_tn(normed_input_all, own_all[:, :q])
    grad_mi = dot_tn(normed_input_all, own_all[:, q : q + x])
    grad_mg = dot_tn(normed_input_all, own_all[:, q + x : q + 2 * x])
    grad_step = dot_tn(normed_input_all, own_all[:, q + 2 * x :])[:, :heads]
    kw = kv_width
    grad_key = dot_tn(normed_input_all, shared_all[:, :kw])
    grad_value = dot_tn(normed_input_all, shared_all[:, kw : 2 * kw])
    grad_si = dot_tn(normed_input_all, shared_all[:, 2 * kw : 2 * kw + ns])
    grad_so = dot_tn(normed_input_all, shared_all[:, 2 * kw + ns :])
    return (
        block_output[None],
        input_grad[None],
        summed[None, :d],
        grad_query[None],
        grad_key[None],
        grad_value[None],
        grad_out[None],
        grad_mg[None],
        grad_mi[None],
        grad_si[None],
        grad_so[None],
        grad_step[None],
        three[0:1],
        three[1:2],
        three[2:3],
        grad_mo[None],
        summed[None, d : 2 * d],
        grad_gate[None],
        grad_up[None],
        grad_down[None],
    )


def solution(mesh):
    rows = P("dp", None)
    by_section = P("section", None)
    split_last = P("section", None, "tensor")
    split_first = P("section", "tensor", None)
    copied = P("section", None, None)
    vector = P("section", "tensor")

    def flat(*args):
        outs = list(shards(*args))
        return tuple(outs)

    return jax.shard_map(
        flat,
        mesh=mesh,
        in_specs=(
            rows,
            rows,
            P("dp"),
            by_section,
            split_last,
            copied,
            copied,
            split_first,
            split_last,
            split_last,
            copied,
            copied,
            split_last,
            vector,
            vector,
            vector,
            split_first,
            by_section,
            split_last,
            split_last,
            split_first,
        ),
        out_specs=(
            P("section", "dp", None),
            P("section", "dp", None),
            by_section,
            split_last,
            copied,
            copied,
            split_first,
            split_last,
            split_last,
            copied,
            copied,
            split_last,
            vector,
            vector,
            vector,
            split_first,
            by_section,
            split_last,
            split_last,
            split_first,
        ),
        check_vma=False,
    )
```
